32 devices in a mesh: row: 4 (over y, x), col: 8 (over z, core).
Axes of the slice: x: 2, y: 2, z: 4, core: 2. Of those that a mesh axis runs over, the one named last changes fastest.
Arguments:
- inverse: float32 [24576, 24576], P('row', 'col'), may hold values from -0.0546875 to 0.0546875
- parent_panel: float32 [24576, 256], P(('row', 'col')), may hold values from -1.8 to 1.8
- child_panel: float32 [24576, 256], P(('row', 'col')), may hold values from -1.8 to 1.8
- child_top: float32 [256, 256], replicated, may hold values from -0.375 to 0.375
- diag_parent: float32 [256, 256], replicated, may hold values from -12 to 12
- diag_child: float32 [256, 256], replicated, may hold values from -12 to 12
- parent_blocks: int32 [192], replicated, may hold values from 0 to 1
- child_blocks: int32 [192], replicated, may hold values from 0 to 1, as said below
Outputs:
- parent_column: float32 [24576, 256], P(('row', 'col'))
- parent_diagonal: float32 [256, 256], replicated
- child_column: float32 [24576, 256], P(('row', 'col'))
- child_upper: float32 [256, 256], replicated
- child_diagonal: float32 [256, 256], replicated
The draws below stay inside these ranges and needn't reach their ends.
Inputs may be any that keep to these rules, and one draw needn't show every extreme that they name: `child_blocks`: each entry is 0 or 1, and is 1 only where parent_blocks is 1.
All inputs are finite; a program needn't handle non-finite values.
Results may differ from the reference program's by a relative error of at most 0.000086.
Values sent between devices are 32-bit elements; how exact they have to be, the bound alone decides.
A program may use at most 192 MiB of HBM per device.

```python
import jax
import jax.numpy as jnp
from jax import lax

M = 24576
W = 256
BLK = 128
NBLK = 192


def structure_flags(key):
    base_key = jax.random.fold_in(key, 11)
    first_key, second_key = jax.random.split(base_key)
    parent_flags = jnp.where(jax.random.randint(first_key, (NBLK,), 0, 3) > 0, 1, 0).astype(jnp.int32)
    keep_flags = jax.random.randint(second_key, (NBLK,), 0, 2).astype(jnp.int32)
    return (parent_flags, parent_flags * keep_flags)


def draw_parent_blocks(key, part):
    return structure_flags(key)[0]


def draw_child_blocks(key, part):
    return structure_flags(key)[1]


def spiked(drawn, stream_key, source, target, parts, factor):
    owner, partner = [(jnp.arange(drawn.shape[position]) // (drawn.shape[position] // parts)).reshape([-1 if axis == position else 1 for axis in range(drawn.ndim)]) for position in (source, target)]
    chosen = jax.random.permutation(stream_key, parts)[partner]
    strong = (owner == chosen) | (owner == (partner + parts // 2) % parts)
    return jnp.where(strong, factor * drawn, drawn)


def level_of(own_key, shape, pieces, smallest, high):
    def one(axis_at, parts):
        steps = jax.random.uniform(jax.random.fold_in(jax.random.fold_in(own_key, 6), axis_at), (parts,), jnp.float32, smallest / len(pieces), high / len(pieces))
        return jnp.repeat(jnp.exp(steps), shape[axis_at] // parts).reshape((-1,) + (1,) * (len(shape) - axis_at - 1))

    level = one(*pieces[0])
    for cut in pieces[1:]:
        level = level * one(*cut)
    return level


def bell_draw(stream_key, shape, spread, limit, pieces=(), dtype=jnp.bfloat16):
    factor_of = level_of(stream_key, shape, pieces, -0.22, 0.18) if pieces else 1.0
    entries = jax.random.normal(stream_key, shape, jnp.float32) * spread * factor_of
    return jnp.minimum(jnp.maximum(entries, -limit), limit).astype(dtype)


def noise_with(own_key, dims, scale, reach, cuts, heavy, kind=jnp.bfloat16):
    result = scale * jax.random.normal(own_key, dims, jnp.float32)
    if cuts:
        result = result * level_of(own_key, dims, cuts, -0.22, 0.18)
    return jnp.clip(spiked(result, jax.random.fold_in(own_key, 3), *heavy), -reach, reach).astype(kind)


def setup_inputs(seed: int = 0) -> dict:
    key_of = jax.random.split(jax.random.key(seed), 9)
    inverse = noise_with(key_of[0], (M, M), M ** -0.5, 0.0546875, ((0, 4), (1, 8)), (1, 0, 8, 2.0), jnp.float32)
    parent_panel = bell_draw(key_of[1], (M, W), 0.3, 1.8, ((0, 32),), jnp.float32)
    child_panel = bell_draw(key_of[2], (M, W), 0.3, 1.8, ((0, 32),), jnp.float32)
    child_top = bell_draw(key_of[3], (W, W), W ** -0.5, 0.375, (), jnp.float32)
    diag_parent = bell_draw(key_of[4], (W, W), 2.0, 12.0, (), jnp.float32)
    diag_child = bell_draw(key_of[5], (W, W), 2.0, 12.0, (), jnp.float32)
    parent_blocks = draw_parent_blocks(jax.random.fold_in(key_of[8], 71), 0)
    child_blocks = draw_child_blocks(jax.random.fold_in(key_of[8], 71), 0)
    return dict(inverse=inverse, parent_panel=parent_panel, child_panel=child_panel, child_top=child_top, diag_parent=diag_parent, diag_child=diag_child, parent_blocks=parent_blocks, child_blocks=child_blocks)


def expand_mask(blocks):
    flags = jnp.repeat(blocks, BLK, total_repeat_length=blocks.shape[0] * BLK)
    return flags.astype(jnp.float32)[:, None]


def matmul(left, right):
    return jnp.dot(left, right, precision=lax.Precision.HIGHEST, preferred_element_type=jnp.float32)


def reference(inverse, parent_panel, child_panel, child_top, diag_parent, diag_child, parent_blocks, child_blocks):
    parent_mask = expand_mask(parent_blocks)
    child_mask = expand_mask(child_blocks)
    parent_masked = parent_panel * parent_mask
    child_masked = child_panel * child_mask
    parent_image = matmul(inverse, parent_masked)
    child_image = matmul(inverse, child_masked)
    parent_column = -(parent_mask * parent_image)
    parent_diagonal = diag_parent - matmul(parent_masked.T, parent_column)
    child_column = -(child_mask * (matmul(parent_column, child_top) + child_image))
    child_upper = -(matmul(parent_diagonal, child_top) + matmul(parent_column.T, child_masked))
    child_diagonal = diag_child - matmul(child_top.T, child_upper) - matmul(child_masked.T, child_column)
    return parent_column, parent_diagonal, child_column, child_upper, child_diagonal
```

```python
import functools

import jax
import jax.numpy as jnp
from jax import lax
from jax.experimental import pallas as pl
from jax.experimental.pallas import tpu as pltpu
from jax.sharding import PartitionSpec as P

BLK = 128
GROUP = 4
BOTH = ("row", "col")


def matmul(left, right):
    return jnp.dot(
        left, right, precision=lax.Precision.HIGH, preferred_element_type=jnp.float32
    )


def local_mask(blocks, rows_here):
    flags = jnp.broadcast_to(blocks[:, None], (blocks.shape[0], BLK)).reshape(-1)
    device = lax.axis_index("row") * lax.axis_size("col") + lax.axis_index("col")
    return lax.dynamic_slice_in_dim(flags, device * rows_here, rows_here, 0)[:, None] > 0


def product_kernel(
    row_flags, col_flags, inverse, panel, out, rows, cols, held, high, low, total, in_sems, out_sems
):
    def listed(flags, places):
        def step(i, count):
            places[count] = i
            return count + flags[i]

        return lax.fori_loop(0, flags.shape[0], step, 0)

    n_rows = listed(row_flags, rows)
    n_cols = listed(col_flags, cols)
    groups = (n_rows + GROUP - 1) // GROUP
    pairs = (n_cols + 1) // 2

    def fetch(group, q, slot):
        place = rows[jnp.minimum(group * GROUP + q, n_rows - 1)]
        return pltpu.make_async_copy(
            inverse.at[pl.ds(pl.multiple_of(place * BLK, BLK), BLK), :],
            held.at[slot, pl.ds(q * BLK, BLK), :],
            in_sems.at[slot, q],
        )

    def put(group, q, slot):
        place = rows[jnp.minimum(group * GROUP + q, n_rows - 1)]
        return pltpu.make_async_copy(
            total.at[slot, pl.ds(q * BLK, BLK), :],
            out.at[pl.ds(pl.multiple_of(place * BLK, BLK), BLK), :],
            out_sems.at[slot, q],
        )

    def each(group, act):
        for q in range(GROUP):

            @pl.when((group >= 0) & (group * GROUP + q < n_rows))
            def _():
                act(q)

    each(0, lambda q: fetch(0, q, 0).start())

    def split(t, carry):
        place = pl.multiple_of(cols[t] * BLK, BLK)
        block = panel[pl.ds(place, BLK), :]
        top = block.astype(jnp.bfloat16)
        here = pl.ds(pl.multiple_of(t * BLK, BLK), BLK)
        high[here, :] = top
        low[here, :] = (block - top.astype(jnp.float32)).astype(jnp.bfloat16)
        return carry

    lax.fori_loop(0, n_cols, split, 0)
    tail = pl.ds(pl.multiple_of(n_cols * BLK, BLK), BLK)
    high[tail, :] = jnp.zeros((BLK, high.shape[1]), jnp.bfloat16)
    low[tail, :] = jnp.zeros((BLK, low.shape[1]), jnp.bfloat16)
    cols[n_cols] = 0

    def one_group(group, carry):
        slot = lax.rem(group, 2)
        each(group + 1, lambda q: fetch(group + 1, q, 1 - slot).start())
        each(group - 2, lambda q: put(group - 2, q, slot).wait())
        each(group, lambda q: fetch(group, q, slot).wait())
        total[slot] = jnp.zeros(total.shape[1:], jnp.float32)

        def one_pair(pair, inner):
            first = pl.multiple_of(cols[2 * pair] * BLK, BLK)
            second = pl.multiple_of(cols[2 * pair + 1] * BLK, BLK)
            left = jnp.concatenate(
                [held[slot, :, pl.ds(first, BLK)], held[slot, :, pl.ds(second, BLK)]], axis=1
            )
            left_high = left.astype(jnp.bfloat16)
            left_low = (left - left_high.astype(jnp.float32)).astype(jnp.bfloat16)
            here = pl.ds(pl.multiple_of(pair * 2 * BLK, 2 * BLK), 2 * BLK)
            right_high = high[here, :]
            right_low = low[here, :]
            dot = functools.partial(jnp.dot, preferred_element_type=jnp.float32)
            total[slot] += (
                dot(left_high, right_high) + dot(left_low, right_high) + dot(left_high, right_low)
            )
            return inner

        lax.fori_loop(0, pairs, one_pair, 0)
        each(group, lambda q: put(group, q, slot).start())
        return carry

    lax.fori_loop(0, groups, one_group, 0)
    for back in (2, 1):
        last = groups - back
        each(last, lambda q: put(last, q, lax.rem(jnp.maximum(last, 0), 2)).wait())


def product(inverse, panel, blocks):
    height, width = inverse.shape
    tall, wide = height // BLK, width // BLK
    row_flags = lax.dynamic_slice_in_dim(blocks, lax.axis_index("row") * tall, tall, 0)
    col_flags = lax.dynamic_slice_in_dim(blocks, lax.axis_index("col") * wide, wide, 0)
    across = panel.shape[1]
    return pl.pallas_call(
        product_kernel,
        out_shape=jax.ShapeDtypeStruct((height, across), jnp.float32),
        in_specs=[
            pl.BlockSpec(memory_space=pltpu.SMEM),
            pl.BlockSpec(memory_space=pltpu.SMEM),
            pl.BlockSpec(memory_space=pl.ANY),
            pl.BlockSpec(memory_space=pltpu.VMEM),
        ],
        out_specs=pl.BlockSpec(memory_space=pl.ANY),
        scratch_shapes=[
            pltpu.SMEM((tall + 1,), jnp.int32),
            pltpu.SMEM((wide + 1,), jnp.int32),
            pltpu.VMEM((2, GROUP * BLK, width), jnp.float32),
            pltpu.VMEM((width + BLK, across), jnp.bfloat16),
            pltpu.VMEM((width + BLK, across), jnp.bfloat16),
            pltpu.VMEM((2, GROUP * BLK, across), jnp.float32),
            pltpu.SemaphoreType.DMA((2, GROUP)),
            pltpu.SemaphoreType.DMA((2, GROUP)),
        ],
        compiler_params=pltpu.CompilerParams(vmem_limit_bytes=40 * 2**20),
        cost_estimate=pl.CostEstimate(
            flops=3 * height * width * across, bytes_accessed=height * width * 2, transcendentals=0
        ),
    )(row_flags, col_flags, inverse, panel)


def column_rows(panel):
    n_row, n_col = lax.axis_size("row"), lax.axis_size("col")
    routes = [(k, k % n_row * n_col + k // n_row) for k in range(n_row * n_col)]
    moved = lax.ppermute(panel, BOTH, routes)
    return lax.all_gather(moved, "row", axis=0, tiled=True)


def summed_rows(partial, rows_here):
    n_col = lax.axis_size("col")
    chips = n_col // 2
    index = lax.axis_index("col")
    chip, core = index // 2, index % 2
    step = 1 - 2 * core
    parts = partial.reshape(chips, 2, rows_here, partial.shape[1])
    theirs = lax.dynamic_index_in_dim(parts, 1 - core, 1, keepdims=False)
    mine = lax.dynamic_index_in_dim(parts, core, 1, keepdims=False)
    got = lax.ppermute(theirs, "col", [(k, k ^ 1) for k in range(n_col)])
    ring = [((2 * z + c), (z + 1 - 2 * c) % chips * 2 + c) for z in range(chips) for c in (0, 1)]

    def term(s):
        place = (chip - step * (s + 1) + 2 * chips * (s + 1)) % chips
        return lax.dynamic_index_in_dim(mine, place, 0, keepdims=False) + (
            lax.dynamic_index_in_dim(got, place, 0, keepdims=False)
        )

    running = term(0)
    for s in range(1, chips):
        running = lax.ppermute(running, "col", ring) + term(s)
    return running


def total_of(value):
    devices = lax.axis_size("row") * lax.axis_size("col")
    bit = 1
    while bit < devices:
        value = value + lax.ppermute(value, BOTH, [(k, k ^ bit) for k in range(devices)])
        bit *= 2
    return value


def per_device(
    inverse,
    parent_panel,
    child_panel,
    child_top,
    diag_parent,
    diag_child,
    parent_blocks,
    child_blocks,
):
    rows_here = parent_panel.shape[0]
    parent_mask = local_mask(parent_blocks, rows_here)
    child_mask = local_mask(child_blocks, rows_here)
    parent_masked = jnp.where(parent_mask, parent_panel, 0)
    child_masked = jnp.where(child_mask, child_panel, 0)
    parent_rows = column_rows(parent_panel)
    child_rows = column_rows(child_panel)
    parent_partial = product(inverse, parent_rows, parent_blocks)
    child_partial = product(inverse, child_rows, child_blocks)
    parent_column = jnp.where(parent_mask, -summed_rows(parent_partial, rows_here), 0)
    child_image = jnp.where(child_mask, summed_rows(child_partial, rows_here), 0)
    parent_local = matmul(parent_masked.T, parent_column)
    cross_local = matmul(parent_column.T, child_masked)
    carried = matmul(parent_column, child_top)
    child_column = jnp.where(child_mask, -(carried + child_image), 0)
    image_local = matmul(child_masked.T, child_image)
    first_sums = total_of(jnp.stack([parent_local, cross_local]))
    parent_sum, cross_sum = first_sums[0], first_sums[1]
    image_sum = total_of(image_local)
    parent_diagonal = diag_parent - parent_sum
    child_upper = -(matmul(parent_diagonal, child_top) + cross_sum)
    child_diagonal = (
        diag_child - matmul(child_top.T, child_upper) + matmul(cross_sum.T, child_top) + image_sum
    )
    return (parent_column, parent_diagonal, child_column, child_upper, child_diagonal)


def solution(mesh):
    placed = (
        P("row", "col"),
        P(("row", "col"), None),
        P(("row", "col"), None),
        P(),
        P(),
        P(),
        P(),
        P(),
    )
    return jax.shard_map(
        per_device,
        mesh=mesh,
        in_specs=placed,
        out_specs=(P(("row", "col"), None), P(), P(("row", "col"), None), P(), P()),
        check_vma=False,
    )
```

```python
import functools

import jax
import jax.numpy as jnp
from jax import lax
from jax.experimental import pallas as pl
from jax.experimental.pallas import tpu as pltpu
from jax.sharding import PartitionSpec as P

BLK = 128
GROUP = 4
BOTH = ("row", "col")


def matmul(left, right):
    return jnp.dot(
        left, right, precision=lax.Precision.HIGH, preferred_element_type=jnp.float32
    )


def local_mask(blocks, rows_here):
    flags = jnp.broadcast_to(blocks[:, None], (blocks.shape[0], BLK)).reshape(-1)
    device = lax.axis_index("row") * lax.axis_size("col") + lax.axis_index("col")
    return lax.dynamic_slice_in_dim(flags, device * rows_here, rows_here, 0)[:, None] > 0


def product_kernel(
    row_flags, col_flags, inverse, panel, out, rows, cols, held, high, low, total, in_sems, out_sems
):
    def listed(flags, places):
        def step(i, count):
            places[count] = i
            return count + flags[i]

        return lax.fori_loop(0, flags.shape[0], step, 0)

    n_rows = listed(row_flags, rows)
    n_cols = listed(col_flags, cols)
    groups = (n_rows + GROUP - 1) // GROUP
    pairs = (n_cols + 1) // 2

    def fetch(group, q, slot):
        place = rows[jnp.minimum(group * GROUP + q, n_rows - 1)]
        return pltpu.make_async_copy(
            inverse.at[pl.ds(pl.multiple_of(place * BLK, BLK), BLK), :],
            held.at[slot, pl.ds(q * BLK, BLK), :],
            in_sems.at[slot, q],
        )

    def put(group, q, slot):
        place = rows[jnp.minimum(group * GROUP + q, n_rows - 1)]
        return pltpu.make_async_copy(
            total.at[slot, pl.ds(q * BLK, BLK), :],
            out.at[pl.ds(pl.multiple_of(place * BLK, BLK), BLK), :],
            out_sems.at[slot, q],
        )

    def each(group, act):
        for q in range(GROUP):

            @pl.when((group >= 0) & (group * GROUP + q < n_rows))
            def _():
                act(q)

    each(0, lambda q: fetch(0, q, 0).start())

    def split(t, carry):
        place = pl.multiple_of(cols[t] * BLK, BLK)
        block = panel[pl.ds(place, BLK), :]
        top = block.astype(jnp.bfloat16)
        here = pl.ds(pl.multiple_of(t * BLK, BLK), BLK)
        high[here, :] = top
        low[here, :] = (block - top.astype(jnp.float32)).astype(jnp.bfloat16)
        return carry

    lax.fori_loop(0, n_cols, split, 0)
    tail = pl.ds(pl.multiple_of(n_cols * BLK, BLK), BLK)
    high[tail, :] = jnp.zeros((BLK, high.shape[1]), jnp.bfloat16)
    low[tail, :] = jnp.zeros((BLK, low.shape[1]), jnp.bfloat16)
    cols[n_cols] = 0

    def one_group(group, carry):
        slot = lax.rem(group, 2)
        each(group + 1, lambda q: fetch(group + 1, q, 1 - slot).start())
        each(group - 2, lambda q: put(group - 2, q, slot).wait())
        each(group, lambda q: fetch(group, q, slot).wait())
        total[slot] = jnp.zeros(total.shape[1:], jnp.float32)

        def one_pair(pair, inner):
            first = pl.multiple_of(cols[2 * pair] * BLK, BLK)
            second = pl.multiple_of(cols[2 * pair + 1] * BLK, BLK)
            left = jnp.concatenate(
                [held[slot, :, pl.ds(first, BLK)], held[slot, :, pl.ds(second, BLK)]], axis=1
            )
            left_high = left.astype(jnp.bfloat16)
            left_low = (left - left_high.astype(jnp.float32)).astype(jnp.bfloat16)
            here = pl.ds(pl.multiple_of(pair * 2 * BLK, 2 * BLK), 2 * BLK)
            right_high = high[here, :]
            right_low = low[here, :]
            dot = functools.partial(jnp.dot, preferred_element_type=jnp.float32)
            total[slot] += (
                dot(left_high, right_high) + dot(left_low, right_high) + dot(left_high, right_low)
            )
            return inner

        lax.fori_loop(0, pairs, one_pair, 0)
        each(group, lambda q: put(group, q, slot).start())
        return carry

    lax.fori_loop(0, groups, one_group, 0)
    for back in (2, 1):
        last = groups - back
        each(last, lambda q: put(last, q, lax.rem(jnp.maximum(last, 0), 2)).wait())


def product(inverse, panel, blocks):
    height, width = inverse.shape
    tall, wide = height // BLK, width // BLK
    row_flags = lax.dynamic_slice_in_dim(blocks, lax.axis_index("row") * tall, tall, 0)
    col_flags = lax.dynamic_slice_in_dim(blocks, lax.axis_index("col") * wide, wide, 0)
    across = panel.shape[1]
    return pl.pallas_call(
        product_kernel,
        out_shape=jax.ShapeDtypeStruct((height, across), jnp.float32),
        in_specs=[
            pl.BlockSpec(memory_space=pltpu.SMEM),
            pl.BlockSpec(memory_space=pltpu.SMEM),
            pl.BlockSpec(memory_space=pl.ANY),
            pl.BlockSpec(memory_space=pltpu.VMEM),
        ],
        out_specs=pl.BlockSpec(memory_space=pl.ANY),
        scratch_shapes=[
            pltpu.SMEM((tall + 1,), jnp.int32),
            pltpu.SMEM((wide + 1,), jnp.int32),
            pltpu.VMEM((2, GROUP * BLK, width), jnp.float32),
            pltpu.VMEM((width + BLK, across), jnp.bfloat16),
            pltpu.VMEM((width + BLK, across), jnp.bfloat16),
            pltpu.VMEM((2, GROUP * BLK, across), jnp.float32),
            pltpu.SemaphoreType.DMA((2, GROUP)),
            pltpu.SemaphoreType.DMA((2, GROUP)),
        ],
        compiler_params=pltpu.CompilerParams(vmem_limit_bytes=40 * 2**20),
        cost_estimate=pl.CostEstimate(
            flops=3 * height * width * across, bytes_accessed=height * width * 2, transcendentals=0
        ),
    )(row_flags, col_flags, inverse, panel)


def routed(panel):
    n_row, n_col = lax.axis_size("row"), lax.axis_size("col")
    routes = [(k, k % n_row * n_col + k // n_row) for k in range(n_row * n_col)]
    return lax.ppermute(panel, BOTH, routes)


def gathered(moved):
    return lax.all_gather(moved, "row", axis=0, tiled=True)


def summed_rows(partial, rows_here):
    n_col = lax.axis_size("col")
    chips = n_col // 2
    index = lax.axis_index("col")
    chip, core = index // 2, index % 2
    step = 1 - 2 * core
    swap = [(k, k ^ 1) for k in range(n_col)]
    ring = [((2 * z + c), (z + 1 - 2 * c) % chips * 2 + c) for z in range(chips) for c in (0, 1)]

    def part(place, side):
        start = (lax.rem(place + 2 * chips, chips) * 2 + side) * rows_here
        return lax.dynamic_slice_in_dim(partial, start, rows_here, 0)

    got = []
    for s in range(chips):
        got.append(lax.ppermute(part(chip + step * ((s + 1) % chips), 1 - core), "col", swap))

    def term(s):
        return part(chip - step * ((s + 1) % chips), core) + got[s]

    running = term(0)
    for s in range(1, chips):
        running = lax.ppermute(running, "col", ring) + term(s)
    return running


def sum_kernel(value, out, got_col, got_row, middle, sent_col, came_col, sent_row, came_row):
    n_col, n_row = value.shape[0], value.shape[1]
    row, col = lax.axis_index("row"), lax.axis_index("col")
    mesh_ids = pl.DeviceIdType.MESH

    barrier = pltpu.get_barrier_semaphore()
    for k in range(1, n_col):
        pl.semaphore_signal(
            barrier, inc=1, device_id=(row, lax.rem(col + k, n_col)), device_id_type=mesh_ids
        )
    for k in range(1, n_row):
        pl.semaphore_signal(
            barrier, inc=1, device_id=(lax.rem(row + k, n_row), col), device_id_type=mesh_ids
        )
    pl.semaphore_wait(barrier, n_col + n_row - 2)

    def along_col(phase, source, target):
        copies = []
        for k in range(1, n_col):
            there = lax.rem(col + k, n_col)
            copies.append(
                pltpu.make_async_remote_copy(
                    src_ref=source(there),
                    dst_ref=target(k),
                    send_sem=sent_col.at[phase, k],
                    recv_sem=came_col.at[phase, k],
                    device_id=(row, there),
                    device_id_type=mesh_ids,
                )
            )
        for copy in copies:
            copy.start()
        for copy in copies:
            copy.wait()

    def along_row(phase, source, target):
        copies = []
        for k in range(1, n_row):
            there = lax.rem(row + k, n_row)
            copies.append(
                pltpu.make_async_remote_copy(
                    src_ref=source(there),
                    dst_ref=target(k),
                    send_sem=sent_row.at[phase, k],
                    recv_sem=came_row.at[phase, k],
                    device_id=(there, col),
                    device_id_type=mesh_ids,
                )
            )
        for copy in copies:
            copy.start()
        for copy in copies:
            copy.wait()

    along_col(0, lambda there: value.at[there], lambda k: got_col.at[k])
    summed = value[col]
    for k in range(1, n_col):
        summed += got_col[k]
    middle[...] = summed
    along_row(0, lambda there: middle.at[there], lambda k: got_row.at[k])
    final = middle[row]
    for k in range(1, n_row):
        final += got_row[k]
    out[col, row] = final
    along_row(1, lambda there: out.at[col, row], lambda k: out.at[col, row])
    along_col(1, lambda there: out.at[col], lambda k: out.at[col])


def total_of(value):
    n_row, n_col = lax.axis_size("row"), lax.axis_size("col")
    across = value.shape[-1]
    each = value.size // (n_row * n_col * across)
    shape = (n_col, n_row, each, across)
    summed = pl.pallas_call(
        sum_kernel,
        out_shape=jax.ShapeDtypeStruct(shape, jnp.float32),
        in_specs=[pl.BlockSpec(memory_space=pltpu.VMEM)],
        out_specs=pl.BlockSpec(memory_space=pltpu.VMEM),
        scratch_shapes=[
            pltpu.VMEM(shape, jnp.float32),
            pltpu.VMEM(shape[1:], jnp.float32),
            pltpu.VMEM(shape[1:], jnp.float32),
            pltpu.SemaphoreType.DMA((2, n_col)),
            pltpu.SemaphoreType.DMA((2, n_col)),
            pltpu.SemaphoreType.DMA((2, n_row)),
            pltpu.SemaphoreType.DMA((2, n_row)),
        ],
        compiler_params=pltpu.CompilerParams(collective_id=0, has_side_effects=True),
    )(value.reshape(shape))
    return summed.reshape(value.shape)


def per_device(
    inverse,
    parent_panel,
    child_panel,
    child_top,
    diag_parent,
    diag_child,
    parent_blocks,
    child_blocks,
):
    rows_here = parent_panel.shape[0]
    parent_mask = local_mask(parent_blocks, rows_here)
    child_mask = local_mask(child_blocks, rows_here)
    parent_masked = jnp.where(parent_mask, parent_panel, 0)
    child_masked = jnp.where(child_mask, child_panel, 0)
    parent_moved = routed(parent_panel)
    parent_moved, child_panel_later = lax.optimization_barrier((parent_moved, child_panel))
    parent_rows = gathered(parent_moved)
    child_rows = gathered(routed(child_panel_later))
    parent_partial = product(inverse, parent_rows, parent_blocks)
    child_partial = product(inverse, child_rows, child_blocks)
    parent_column = jnp.where(parent_mask, -summed_rows(parent_partial, rows_here), 0)
    child_image = jnp.where(child_mask, summed_rows(child_partial, rows_here), 0)
    parent_local = matmul(parent_masked.T, parent_column)
    cross_local = matmul(parent_column.T, child_masked)
    carried = matmul(parent_column, child_top)
    child_column = jnp.where(child_mask, -(carried + child_image), 0)
    image_local = matmul(child_masked.T, child_image)
    sums = total_of(jnp.stack([parent_local, cross_local, image_local]))
    parent_sum, cross_sum, image_sum = sums[0], sums[1], sums[2]
    parent_diagonal = diag_parent - parent_sum
    child_upper = -(matmul(parent_diagonal, child_top) + cross_sum)
    child_diagonal = (
        diag_child - matmul(child_top.T, child_upper) + matmul(cross_sum.T, child_top) + image_sum
    )
    return (parent_column, parent_diagonal, child_column, child_upper, child_diagonal)


def solution(mesh):
    placed = (
        P("row", "col"),
        P(("row", "col"), None),
        P(("row", "col"), None),
        P(),
        P(),
        P(),
        P(),
        P(),
    )
    return jax.shard_map(
        per_device,
        mesh=mesh,
        in_specs=placed,
        out_specs=(P(("row", "col"), None), P(), P(("row", "col"), None), P(), P()),
        check_vma=False,
    )
```

```python
import functools

import jax
import jax.numpy as jnp
from jax import lax
from jax.experimental import pallas as pl
from jax.experimental.pallas import tpu as pltpu
from jax.sharding import PartitionSpec as P

BLK = 128
GROUP = 4
BOTH = ("row", "col")


def matmul(left, right):
    return jnp.dot(
        left, right, precision=lax.Precision.HIGH, preferred_element_type=jnp.float32
    )


def local_mask(blocks, rows_here):
    flags = jnp.broadcast_to(blocks[:, None], (blocks.shape[0], BLK)).reshape(-1)
    device = lax.axis_index("row") * lax.axis_size("col") + lax.axis_index("col")
    return lax.dynamic_slice_in_dim(flags, device * rows_here, rows_here, 0)[:, None] > 0


def product_kernel(
    row_flags, col_flags, inverse, panel, out, rows, cols, held, high, low, total, in_sems, out_sems
):
    def listed(flags, places):
        def step(i, count):
            places[count] = i
            return count + flags[i]

        return lax.fori_loop(0, flags.shape[0], step, 0)

    n_rows = listed(row_flags, rows)
    n_cols = listed(col_flags, cols)
    groups = (n_rows + GROUP - 1) // GROUP
    pairs = (n_cols + 1) // 2

    def fetch(group, q, slot):
        place = rows[jnp.minimum(group * GROUP + q, n_rows - 1)]
        return pltpu.make_async_copy(
            inverse.at[pl.ds(pl.multiple_of(place * BLK, BLK), BLK), :],
            held.at[slot, pl.ds(q * BLK, BLK), :],
            in_sems.at[slot, q],
        )

    def put(group, q, slot):
        place = rows[jnp.minimum(group * GROUP + q, n_rows - 1)]
        return pltpu.make_async_copy(
            total.at[slot, pl.ds(q * BLK, BLK), :],
            out.at[pl.ds(pl.multiple_of(place * BLK, BLK), BLK), :],
            out_sems.at[slot, q],
        )

    def each(group, act):
        for q in range(GROUP):

            @pl.when((group >= 0) & (group * GROUP + q < n_rows))
            def _():
                act(q)

    each(0, lambda q: fetch(0, q, 0).start())

    def split(t, carry):
        place = pl.multiple_of(cols[t] * BLK, BLK)
        block = panel[pl.ds(place, BLK), :]
        top = block.astype(jnp.bfloat16)
        here = pl.ds(pl.multiple_of(t * BLK, BLK), BLK)
        high[here, :] = top
        low[here, :] = (block - top.astype(jnp.float32)).astype(jnp.bfloat16)
        return carry

    lax.fori_loop(0, n_cols, split, 0)
    tail = pl.ds(pl.multiple_of(n_cols * BLK, BLK), BLK)
    high[tail, :] = jnp.zeros((BLK, high.shape[1]), jnp.bfloat16)
    low[tail, :] = jnp.zeros((BLK, low.shape[1]), jnp.bfloat16)
    cols[n_cols] = 0

    def one_group(group, carry):
        slot = lax.rem(group, 2)
        each(group + 1, lambda q: fetch(group + 1, q, 1 - slot).start())
        each(group - 2, lambda q: put(group - 2, q, slot).wait())
        each(group, lambda q: fetch(group, q, slot).wait())
        total[slot] = jnp.zeros(total.shape[1:], jnp.float32)

        def one_pair(pair, inner):
            first = pl.multiple_of(cols[2 * pair] * BLK, BLK)
            second = pl.multiple_of(cols[2 * pair + 1] * BLK, BLK)
            left = jnp.concatenate(
                [held[slot, :, pl.ds(first, BLK)], held[slot, :, pl.ds(second, BLK)]], axis=1
            )
            left_high = left.astype(jnp.bfloat16)
            left_low = (left - left_high.astype(jnp.float32)).astype(jnp.bfloat16)
            here = pl.ds(pl.multiple_of(pair * 2 * BLK, 2 * BLK), 2 * BLK)
            right_high = high[here, :]
            right_low = low[here, :]
            dot = functools.partial(jnp.dot, preferred_element_type=jnp.float32)
            total[slot] += (
                dot(left_high, right_high) + dot(left_low, right_high) + dot(left_high, right_low)
            )
            return inner

        lax.fori_loop(0, pairs, one_pair, 0)
        each(group, lambda q: put(group, q, slot).start())
        return carry

    lax.fori_loop(0, groups, one_group, 0)
    for back in (2, 1):
        last = groups - back
        each(last, lambda q: put(last, q, lax.rem(jnp.maximum(last, 0), 2)).wait())


def product(inverse, panel, blocks):
    height, width = inverse.shape
    tall, wide = height // BLK, width // BLK
    row_flags = lax.dynamic_slice_in_dim(blocks, lax.axis_index("row") * tall, tall, 0)
    col_flags = lax.dynamic_slice_in_dim(blocks, lax.axis_index("col") * wide, wide, 0)
    across = panel.shape[1]
    return pl.pallas_call(
        product_kernel,
        out_shape=jax.ShapeDtypeStruct((height, across), jnp.float32),
        in_specs=[
            pl.BlockSpec(memory_space=pltpu.SMEM),
            pl.BlockSpec(memory_space=pltpu.SMEM),
            pl.BlockSpec(memory_space=pl.ANY),
            pl.BlockSpec(memory_space=pltpu.VMEM),
        ],
        out_specs=pl.BlockSpec(memory_space=pl.ANY),
        scratch_shapes=[
            pltpu.SMEM((tall + 1,), jnp.int32),
            pltpu.SMEM((wide + 1,), jnp.int32),
            pltpu.VMEM((2, GROUP * BLK, width), jnp.float32),
            pltpu.VMEM((width + BLK, across), jnp.bfloat16),
            pltpu.VMEM((width + BLK, across), jnp.bfloat16),
            pltpu.VMEM((2, GROUP * BLK, across), jnp.float32),
            pltpu.SemaphoreType.DMA((2, GROUP)),
            pltpu.SemaphoreType.DMA((2, GROUP)),
        ],
        compiler_params=pltpu.CompilerParams(vmem_limit_bytes=40 * 2**20),
        cost_estimate=pl.CostEstimate(
            flops=3 * height * width * across, bytes_accessed=height * width * 2, transcendentals=0
        ),
    )(row_flags, col_flags, inverse, panel)


def routed(panel):
    n_row, n_col = lax.axis_size("row"), lax.axis_size("col")
    row, col = lax.axis_index("row"), lax.axis_index("col")
    ratio = n_col // n_row
    piece = panel.shape[0] // n_row

    def pick(pieces, place):
        return lax.dynamic_slice_in_dim(pieces, lax.rem(place + n_row, n_row) * piece, piece, 0)

    across = [pick(panel, row)]
    for k in range(1, n_row):
        lanes = [(r, (r + k) % n_row) for r in range(n_row)]
        across.append(lax.ppermute(pick(panel, row + k), "row", lanes))
    across = jnp.concatenate(across, axis=0)
    along = []
    for m in range(n_row):
        source = lax.rem(col + m, n_row)
        lanes = [(c, ratio * ((c + m) % n_row) + c // n_row) for c in range(n_col)]
        along.append(lax.ppermute(pick(across, row - source), "col", lanes))
    along = jnp.concatenate(along, axis=0)
    return jnp.concatenate([pick(along, col // ratio - j) for j in range(n_row)], axis=0)


def gathered(moved):
    n_row = lax.axis_size("row")
    rows = lax.all_gather(moved, "row", axis=0, tiled=True)
    pieces = rows.reshape(n_row, n_row, moved.shape[0] // n_row, moved.shape[1])
    return pieces.transpose(1, 0, 2, 3).reshape(rows.shape)


def summed_rows(partial, rows_here):
    n_col = lax.axis_size("col")
    chips = n_col // 2
    index = lax.axis_index("col")
    chip, core = index // 2, index % 2
    step = 1 - 2 * core
    swap = [(k, k ^ 1) for k in range(n_col)]
    ring = [((2 * z + c), (z + 1 - 2 * c) % chips * 2 + c) for z in range(chips) for c in (0, 1)]

    def part(place, side):
        start = (lax.rem(place + 2 * chips, chips) * 2 + side) * rows_here
        return lax.dynamic_slice_in_dim(partial, start, rows_here, 0)

    got = []
    for s in range(chips):
        got.append(lax.ppermute(part(chip + step * ((s + 1) % chips), 1 - core), "col", swap))

    def term(s):
        return part(chip - step * ((s + 1) % chips), core) + got[s]

    running = term(0)
    for s in range(1, chips):
        running = lax.ppermute(running, "col", ring) + term(s)
    return running


def sum_kernel(value, out, got_row, got_col, middle, sent_col, came_col, sent_row, came_row):
    n_row, n_col = value.shape[0], value.shape[1]
    row, col = lax.axis_index("row"), lax.axis_index("col")
    mesh_ids = pl.DeviceIdType.MESH

    barrier = pltpu.get_barrier_semaphore()
    for k in range(1, n_col):
        pl.semaphore_signal(
            barrier, inc=1, device_id=(row, lax.rem(col + k, n_col)), device_id_type=mesh_ids
        )
    for k in range(1, n_row):
        pl.semaphore_signal(
            barrier, inc=1, device_id=(lax.rem(row + k, n_row), col), device_id_type=mesh_ids
        )
    pl.semaphore_wait(barrier, n_col + n_row - 2)

    def along_col(phase, source, target):
        copies = []
        for k in range(1, n_col):
            there = lax.rem(col + k, n_col)
            copies.append(
                pltpu.make_async_remote_copy(
                    src_ref=source(there),
                    dst_ref=target(k),
                    send_sem=sent_col.at[phase, k],
                    recv_sem=came_col.at[phase, k],
                    device_id=(row, there),
                    device_id_type=mesh_ids,
                )
            )
        for copy in copies:
            copy.start()
        for copy in copies:
            copy.wait()

    def along_row(phase, source, target):
        copies = []
        for k in range(1, n_row):
            there = lax.rem(row + k, n_row)
            copies.append(
                pltpu.make_async_remote_copy(
                    src_ref=source(there),
                    dst_ref=target(k),
                    send_sem=sent_row.at[phase, k],
                    recv_sem=came_row.at[phase, k],
                    device_id=(there, col),
                    device_id_type=mesh_ids,
                )
            )
        for copy in copies:
            copy.start()
        for copy in copies:
            copy.wait()

    along_row(0, lambda there: value.at[there], lambda k: got_row.at[k])
    summed = value[row]
    for k in range(1, n_row):
        summed += got_row[k]
    middle[...] = summed
    along_col(0, lambda there: middle.at[there], lambda k: got_col.at[k])
    final = middle[col]
    for k in range(1, n_col):
        final += got_col[k]
    out[row, col] = final
    along_col(1, lambda there: out.at[row, col], lambda k: out.at[row, col])
    along_row(1, lambda there: out.at[row], lambda k: out.at[row])


def total_of(value):
    n_row, n_col = lax.axis_size("row"), lax.axis_size("col")
    across = value.shape[-1]
    each = value.size // (n_row * n_col * across)
    shape = (n_row, n_col, each, across)
    summed = pl.pallas_call(
        sum_kernel,
        out_shape=jax.ShapeDtypeStruct(shape, jnp.float32),
        in_specs=[pl.BlockSpec(memory_space=pltpu.VMEM)],
        out_specs=pl.BlockSpec(memory_space=pltpu.VMEM),
        scratch_shapes=[
            pltpu.VMEM(shape, jnp.float32),
            pltpu.VMEM(shape[1:], jnp.float32),
            pltpu.VMEM(shape[1:], jnp.float32),
            pltpu.SemaphoreType.DMA((2, n_col)),
            pltpu.SemaphoreType.DMA((2, n_col)),
            pltpu.SemaphoreType.DMA((2, n_row)),
            pltpu.SemaphoreType.DMA((2, n_row)),
        ],
        compiler_params=pltpu.CompilerParams(collective_id=0, has_side_effects=True),
    )(value.reshape(shape))
    return summed.reshape(value.shape)


def per_device(
    inverse,
    parent_panel,
    child_panel,
    child_top,
    diag_parent,
    diag_child,
    parent_blocks,
    child_blocks,
):
    rows_here = parent_panel.shape[0]
    parent_mask = local_mask(parent_blocks, rows_here)
    child_mask = local_mask(child_blocks, rows_here)
    parent_masked = jnp.where(parent_mask, parent_panel, 0)
    child_masked = jnp.where(child_mask, child_panel, 0)
    parent_moved = routed(parent_panel)
    parent_moved, child_panel_later = lax.optimization_barrier((parent_moved, child_panel))
    parent_rows = gathered(parent_moved)
    child_rows = gathered(routed(child_panel_later))
    parent_partial = product(inverse, parent_rows, parent_blocks)
    child_partial = product(inverse, child_rows, child_blocks)
    parent_column = jnp.where(parent_mask, -summed_rows(parent_partial, rows_here), 0)
    child_image = jnp.where(child_mask, summed_rows(child_partial, rows_here), 0)
    parent_local = matmul(parent_masked.T, parent_column)
    cross_local = matmul(parent_column.T, child_masked)
    carried = matmul(parent_column, child_top)
    child_column = jnp.where(child_mask, -(carried + child_image), 0)
    image_local = matmul(child_masked.T, child_image)
    sums = total_of(jnp.stack([parent_local, cross_local, image_local]))
    parent_sum, cross_sum, image_sum = sums[0], sums[1], sums[2]
    parent_diagonal = diag_parent - parent_sum
    child_upper = -(matmul(parent_diagonal, child_top) + cross_sum)
    child_diagonal = (
        diag_child - matmul(child_top.T, child_upper) + matmul(cross_sum.T, child_top) + image_sum
    )
    return (parent_column, parent_diagonal, child_column, child_upper, child_diagonal)


def solution(mesh):
    placed = (
        P("row", "col"),
        P(("row", "col"), None),
        P(("row", "col"), None),
        P(),
        P(),
        P(),
        P(),
        P(),
    )
    return jax.shard_map(
        per_device,
        mesh=mesh,
        in_specs=placed,
        out_specs=(P(("row", "col"), None), P(), P(("row", "col"), None), P(), P()),
        check_vma=False,
    )
```
